32 devices in a mesh: context: 4 (over z), dp: 4 (over y, x), tensor: 2 (over core).
Axes of the slice: x: 2, y: 2, z: 4, core: 2. Of those that a mesh axis runs over, the one named last changes fastest.
Arguments:
- ssm_input: bfloat16 [4096, 4096], P(('dp', 'context'), 'tensor'), parts along dimension 0, may hold values from -6 to 6
- input_map: bfloat16 [4096, 128], P(('dp', 'context')), parts along dimension 0, may hold values from -0.119628906 to 0.119628906
- output_map: bfloat16 [4096, 128], P(('dp', 'context')), parts along dimension 0, may hold values from -6 to 6
- step_size: float32 [64, 4096], P('tensor', ('dp', 'context')), parts along dimension 1, may hold values from 0.25 to 1
- log_decay: float32 [64, 4096], P('tensor', ('dp', 'context')), parts along dimension 1, may hold values from -1.6 to 0
- skip_gain: float32 [64], P('tensor'), may hold values from 0.5 to 1.5
- norm_gain: float32 [4096], P('tensor'), may hold values from 0.5 to 1.5
- query_weight: bfloat16 [4096, 4096], P('tensor'), may hold values from -0.09375 to 0.09375
- key_states: bfloat16 [4096, 1024], P(('dp', 'context'), 'tensor'), parts along dimension 0, may hold values from -140 to 140
- value_states: bfloat16 [4096, 1024], P(('dp', 'context'), 'tensor'), parts along dimension 0, may hold values from -6 to 6
- block_mask: int32 [32, 8], P('dp'), parts along dimension 0, may hold values 0 or 1
Outputs:
- mixer_out: bfloat16 [4096, 4096], P(('dp', 'context'), 'tensor'), parts along dimension 0
- attended: bfloat16 [4096, 4096], P(('dp', 'context'), 'tensor'), parts along dimension 0
The draws below stay inside these ranges and needn't reach their ends.
There are 4 independent parts, one for each index of `dp`. The reference program is written for one: setup_inputs(seed, part) draws one part's arguments, and reference() takes and returns one part's arrays. A program takes and returns all parts, laid end to end along the dimension named above; an argument that names none is the same for every part. Nothing has to cross between parts.
All inputs are finite; a program needn't handle non-finite values.
Results may differ from the reference program's by a relative error of at most 0.0045.
The reference program's roundings to bfloat16 on the way count: a program that leaves them out, or rounds other values in their place, can miss the bound.
Values may be sent and summed in bfloat16 or wider, within the bound.
A program may use at most 128 MiB of HBM per device.

```python
import math
import jax
import jax.numpy as jnp
from jax import lax

TOK_DEV = 256
SSM_HEADS = 64
HEAD_P = 64
STATE = 128
SPAN = 64
Q_HEADS = 32
KV_HEADS = 8
HEAD_DIM = 128
BLOCK = 128
SEQUENCE_TOKENS = 1024
INNER = 4096
NBLK = 8


def draw_log_decay(key, part):
    stream = jax.random.fold_in(key, 11)
    k_pick, k_slow, k_fast, k_device, k_token, key_positions, key_penalty = jax.random.split(stream, 7)
    share = 0.5
    slow_pick = jax.random.uniform(k_pick, (SSM_HEADS,)) < share
    slow_rate = jnp.exp(jax.random.uniform(k_slow, (SSM_HEADS,), minval=math.log(0.02), maxval=math.log(0.5))) / SEQUENCE_TOKENS
    fast_rate = jnp.exp(jax.random.uniform(k_fast, (SSM_HEADS,), minval=math.log(0.02), maxval=math.log(0.05)))
    head_decay_rate = jnp.where(slow_pick, slow_rate, fast_rate)
    device_factor = jnp.exp(jax.random.uniform(k_device, (SEQUENCE_TOKENS // TOK_DEV,), minval=math.log(0.5), maxval=math.log(2.0)))
    token_multiplier = jnp.exp(jax.random.uniform(k_token, (SSM_HEADS, SEQUENCE_TOKENS), minval=math.log(0.5), maxval=math.log(2.0)))
    dispersion_factor = jnp.repeat(device_factor, TOK_DEV)
    surge_positions = jax.random.randint(key_positions, (2,), 0, SEQUENCE_TOKENS)
    surge_penalty = jax.random.uniform(key_penalty, (2,), minval=0.2, maxval=0.5)
    match_lookup = jnp.arange(SEQUENCE_TOKENS)[:, None] == surge_positions[None, :]
    surge_magnitude = jnp.sum(jnp.where(match_lookup, -jnp.log(1.0 - surge_penalty)[None, :], 0.0), axis=1)
    return -(head_decay_rate[:, None] * dispersion_factor[None, :] * token_multiplier) - surge_magnitude[None, :]


def draw_key_states(key, part):
    stream = jax.random.fold_in(key, 23)
    k_base = jax.random.fold_in(stream, 0)
    shape = (SEQUENCE_TOKENS, KV_HEADS * HEAD_DIM)
    return jnp.clip(jax.random.normal(k_base, shape), -4.0, 4.0).astype(jnp.bfloat16)


def with_ends(result, own_key, smallest, high):
    spot = [jax.random.randint(jax.random.fold_in(own_key, axis), (), 0, length) for axis, length in enumerate(result.shape)]
    main_axis = result.shape.index(max(result.shape))
    next_to = spot[:main_axis] + [(spot[main_axis] + 1) % result.shape[main_axis]] + spot[main_axis + 1:]
    return result.at[tuple(spot)].set(smallest).at[tuple(next_to)].set(high)


def steps_of(stream_key, dims, shards, smallest, largest):
    def one(axis_at, shards_of):
        draws = jax.random.uniform(jax.random.fold_in(jax.random.fold_in(stream_key, 6), axis_at), (shards_of,), jnp.float32, smallest / len(shards), largest / len(shards))
        return jnp.repeat(jnp.exp(draws), dims[axis_at] // shards_of).reshape((-1,) + (1,) * (len(dims) - axis_at - 1))

    factor_of = one(*shards[0])
    for cut in shards[1:]:
        factor_of = factor_of * one(*cut)
    return factor_of


def centred(own_key, dims, spread, limit, cuts=(), held_as=jnp.bfloat16):
    entries = jax.random.normal(own_key, dims, jnp.float32) * spread
    if len(cuts) > 0:
        entries = steps_of(own_key, dims, cuts, -0.22, 0.18) * entries
    return jnp.clip(entries, min=-limit, max=limit).astype(held_as)


def setup_inputs(seed: int = 0, part: int = 0) -> dict:
    keys = jax.random.split(jax.random.key(seed), 12)
    part_keys = jax.random.split(jax.random.fold_in(keys[11], part), 12)
    ssm_input = centred(part_keys[0], (SEQUENCE_TOKENS, INNER), 1.0, 6.0, ((0, 4), (1, 2)))
    input_map = centred(part_keys[1], (SEQUENCE_TOKENS, STATE), 0.02, 0.119628906, ((0, 4),))
    output_map = centred(part_keys[2], (SEQUENCE_TOKENS, STATE), 1.0, 6.0, ((0, 4),))
    step_size = jnp.clip(jnp.exp(math.log(1.0) - 1.3862944 * jax.random.uniform(part_keys[3], (SSM_HEADS, SEQUENCE_TOKENS), jnp.float32) ** steps_of(part_keys[3], (SSM_HEADS, SEQUENCE_TOKENS), ((0, 2), (1, 4)), -0.2, 0.2)), 0.25, 1.0)
    log_decay = draw_log_decay(jax.random.fold_in(jax.random.fold_in(keys[11], part), 71), part)
    skip_gain = jnp.clip(0.5 + 1.0 * jax.random.uniform(keys[5], (SSM_HEADS,), jnp.float32) ** steps_of(keys[5], (SSM_HEADS,), ((0, 2),), -0.2, 0.2), 0.5, 1.5)
    norm_gain = jnp.clip(0.5 + 1.0 * jax.random.uniform(keys[6], (INNER,), jnp.float32) ** steps_of(keys[6], (INNER,), ((0, 2),), -0.2, 0.2), 0.5, 1.5)
    query_weight = centred(keys[7], (INNER, Q_HEADS * HEAD_DIM), INNER ** -0.5, 0.09375, ((0, 2),))
    key_states = draw_key_states(jax.random.fold_in(jax.random.fold_in(keys[11], part), 71), part)
    value_states = centred(part_keys[9], (SEQUENCE_TOKENS, KV_HEADS * HEAD_DIM), 1.0, 6.0, ((0, 4), (1, 2)))
    block_mask = with_ends((jax.random.randint(part_keys[10], (NBLK, NBLK), 0, 2) < 1).astype(jnp.int32), jax.random.fold_in(part_keys[10], 1), 0, 1)
    return {"ssm_input": ssm_input, "input_map": input_map, "output_map": output_map, "step_size": step_size, "log_decay": log_decay, "skip_gain": skip_gain, "norm_gain": norm_gain, "query_weight": query_weight, "key_states": key_states, "value_states": value_states, "block_mask": block_mask}


HIGHEST = lax.Precision.HIGHEST
NEGATIVE = -1e+30

def span_pass(carried, pieces):
    inputs, in_narrow, out_narrow, step_sizes, decays = pieces
    in_wide = in_narrow.astype(jnp.float32)
    out_wide = out_narrow.astype(jnp.float32)
    running = jnp.cumsum(decays, axis=1)
    length = decays.shape[1]
    row_index = lax.broadcasted_iota(jnp.int32, (length, length), 0)
    col_index = lax.broadcasted_iota(jnp.int32, (length, length), 1)
    causal = (row_index >= col_index)[None]
    spread_log = running[:, :, None] - running[:, None, :]
    retain = jnp.where(causal, jnp.exp(jnp.where(causal, spread_log, 0.0)), 0.0)
    intersection = jnp.dot(out_narrow, in_narrow.T, preferred_element_type=jnp.float32)
    weights = intersection[None] * retain * step_sizes[:, None, :]
    y_intra = jnp.einsum('hij,jhp->ihp', weights, inputs, precision=HIGHEST)
    y_inter = jnp.einsum('in,hpn->ihp', out_wide, carried, precision=HIGHEST) * jnp.exp(running).T[:, :, None]
    to_end = jnp.exp(running[:, -1:] - running) * step_sizes
    injected = jnp.einsum('hj,jhp,jn->hpn', to_end, inputs, in_wide, precision=HIGHEST)
    carried = jnp.exp(running[:, -1])[:, None, None] * carried + injected
    return (carried, y_intra + y_inter)

def reference(ssm_input, input_map, output_map, step_size, log_decay, skip_gain, norm_gain, query_weight, key_states, value_states, block_mask):
    length = ssm_input.shape[0]
    span_count = length // SPAN
    inputs = ssm_input.astype(jnp.float32).reshape(length, SSM_HEADS, HEAD_P)
    pieces = (inputs.reshape(span_count, SPAN, SSM_HEADS, HEAD_P), input_map.reshape(span_count, SPAN, STATE), output_map.reshape(span_count, SPAN, STATE), step_size.reshape(SSM_HEADS, span_count, SPAN).transpose(1, 0, 2), log_decay.reshape(SSM_HEADS, span_count, SPAN).transpose(1, 0, 2))
    start_state = jnp.zeros((SSM_HEADS, HEAD_P, STATE), jnp.float32)
    final_state, outputs = lax.scan(span_pass, start_state, pieces)
    scan_out = outputs.reshape(length, SSM_HEADS, HEAD_P) + skip_gain[None, :, None] * inputs
    squares = lax.optimization_barrier(jnp.mean(scan_out * scan_out, axis=-1, keepdims=True))
    normed = scan_out * lax.rsqrt(squares + 1e-05) * norm_gain.reshape(SSM_HEADS, HEAD_P)
    mixer_out = normed.reshape(length, INNER).astype(jnp.bfloat16)
    query = jnp.dot(mixer_out, query_weight, preferred_element_type=jnp.float32).astype(jnp.bfloat16)
    positions = jnp.arange(length, dtype=jnp.int32)
    block_of = positions // BLOCK
    table = block_mask[block_of][:, block_of]
    allowed = (positions[None, :] <= positions[:, None]) & ((table == 1) | (block_of[:, None] == block_of[None, :]))
    group_size = Q_HEADS // KV_HEADS
    score_scale = HEAD_DIM ** (-0.5)

    def one_head(head_index):
        kv_index = head_index // group_size
        q_head = lax.dynamic_slice_in_dim(query, head_index * HEAD_DIM, HEAD_DIM, 1)
        k_head = lax.dynamic_slice_in_dim(key_states, kv_index * HEAD_DIM, HEAD_DIM, 1)
        v_head = lax.dynamic_slice_in_dim(value_states, kv_index * HEAD_DIM, HEAD_DIM, 1)
        scores = jnp.dot(q_head, k_head.T, preferred_element_type=jnp.float32) * score_scale
        scores = jnp.where(allowed, scores, NEGATIVE)
        row_top = lax.optimization_barrier(jnp.max(scores, axis=1, keepdims=True))
        expo_terms = jnp.where(allowed, jnp.exp(scores - row_top), 0.0)
        denominator = lax.optimization_barrier(jnp.sum(expo_terms, axis=1, keepdims=True))
        summed = jnp.dot(expo_terms.astype(jnp.bfloat16), v_head, preferred_element_type=jnp.float32)
        return (summed / denominator).astype(jnp.bfloat16)
    head_outputs = lax.map(one_head, jnp.arange(Q_HEADS, dtype=jnp.int32))
    attended = head_outputs.transpose(1, 0, 2).reshape(length, Q_HEADS * HEAD_DIM)
    return (mixer_out, attended)
```

```python
import functools

import jax
import jax.numpy as jnp
from jax import lax
from jax.experimental import pallas as pl
from jax.experimental.pallas import tpu as pltpu
from jax.sharding import PartitionSpec as P

HEAD_P = 64
STATE = 128
HEAD_DIM = 128
BLOCK = 128
CHUNK = 256
NEGATIVE = -1e30
LOG2E = 1.4426950408889634
HIGHEST = lax.Precision.HIGHEST
MESH = pl.DeviceIdType.MESH
F32 = jnp.float32
BF16 = jnp.bfloat16
NT = (((1,), (1,)), ((), ()))


def split(wide):
    high = wide.astype(BF16)
    return high, (wide - high.astype(F32)).astype(BF16)


def dot(a, b):
    return jnp.dot(a, b, preferred_element_type=F32)


def kernel(
    n,
    mask_ref,
    x_ref,
    b_ref,
    c_ref,
    dt_ref,
    ld_ref,
    skip_ref,
    gain_ref,
    w_ref,
    k_ref,
    v_ref,
    mixer_ref,
    attended_ref,
    kv,
    w_own,
    w_other,
    bt,
    gram,
    col_run,
    col_dt,
    row_run,
    row_dt,
    state,
    arrived,
    mixed,
    mixed_other,
    q_acc,
    q_all,
    bias,
    top,
    total,
    acc,
    kv_send,
    kv_recv,
    st_send,
    st_recv,
    mx_send,
    mx_recv,
    wt_send,
    wt_recv,
    wt_own,
):
    me = lax.axis_index("context")
    core = lax.axis_index("tensor")
    other = 1 - core
    length = x_ref.shape[0]
    chunks = x_ref.shape[1] // CHUNK
    q_cols = w_own.shape[2]
    has_left = me > 0
    has_right = me < n - 1
    heads = q_cols // HEAD_DIM
    group = heads // (k_ref.shape[1] // HEAD_DIM)
    blocks = length // BLOCK

    barrier = pltpu.get_barrier_semaphore()
    pl.semaphore_signal(barrier, inc=1, device_id={"tensor": other}, device_id_type=MESH)

    @pl.when(has_left)
    def _():
        pl.semaphore_signal(barrier, inc=1, device_id={"context": me - 1}, device_id_type=MESH)

    @pl.when(has_right)
    def _():
        pl.semaphore_signal(barrier, inc=1, device_id={"context": me + 1}, device_id_type=MESH)

    peers = 1 + has_left.astype(jnp.int32) + has_right.astype(jnp.int32)
    pl.semaphore_wait(barrier, peers)

    def kv_copy(slot):
        return pltpu.make_async_remote_copy(
            src_ref=kv.at[slot],
            dst_ref=kv.at[slot + 1],
            send_sem=kv_send.at[slot],
            recv_sem=kv_recv.at[slot + 1],
            device_id={"context": me + 1},
            device_id_type=MESH,
        )

    def kv_wait(slot):
        pltpu.make_async_remote_copy(
            src_ref=kv.at[slot - 1],
            dst_ref=kv.at[slot],
            send_sem=kv_send.at[slot - 1],
            recv_sem=kv_recv.at[slot],
            device_id={"context": me - 1},
            device_id_type=MESH,
        ).wait_recv()

    def state_copy(j):
        return pltpu.make_async_remote_copy(
            src_ref=state.at[j],
            dst_ref=arrived.at[j],
            send_sem=st_send.at[j],
            recv_sem=st_recv.at[j],
            device_id={"context": me + 1},
            device_id_type=MESH,
        )

    def mixed_copy(j):
        return pltpu.make_async_remote_copy(
            src_ref=mixed.at[j],
            dst_ref=mixed_other.at[j],
            send_sem=mx_send.at[j],
            recv_sem=mx_recv.at[j],
            device_id={"tensor": other},
            device_id_type=MESH,
        )

    def rows_of(j):
        return pl.ds(pl.multiple_of(j * CHUNK, CHUNK), CHUNK)

    def weight_out(j):
        return pltpu.make_async_remote_copy(
            src_ref=w_ref.at[rows_of(j), pl.ds(pl.multiple_of(other * q_cols, CHUNK), q_cols)],
            dst_ref=w_other.at[j],
            send_sem=wt_send.at[j],
            recv_sem=wt_recv.at[j],
            device_id={"tensor": other},
            device_id_type=MESH,
        )

    def weight_in(j):
        return pltpu.make_async_copy(
            w_ref.at[rows_of(j), pl.ds(pl.multiple_of(core * q_cols, CHUNK), q_cols)],
            w_own.at[j],
            wt_own.at[j],
        )

    kv[0, 0] = k_ref[...]
    kv[0, 1] = v_ref[...]

    @pl.when(has_right)
    def _():
        kv_copy(0).start()

    @pl.loop(0, chunks)
    def _(j):
        weight_in(j).start()
        weight_out(j).start()

    row = lax.broadcasted_iota(jnp.int32, (length, length), 0)
    col = lax.broadcasted_iota(jnp.int32, (length, length), 1)
    causal = row >= col
    tri = jnp.where(causal, 1.0, 0.0).astype(F32)
    eye = jnp.where(row == col, 1.0, 0.0).astype(F32)
    run_rows = lax.dot_general(ld_ref[...], tri, NT, precision=HIGHEST, preferred_element_type=F32)
    run_cols = lax.dot_general(tri, ld_ref[...], NT, precision=HIGHEST, preferred_element_type=F32)
    dt_cols = lax.dot_general(eye, dt_ref[...], NT, precision=HIGHEST, preferred_element_type=F32)
    per = CHUNK // HEAD_P
    for j in range(chunks):
        col_run[j] = run_cols[:, j * per : (j + 1) * per]
        col_dt[j] = dt_cols[:, j * per : (j + 1) * per]
        row_run[j] = run_rows[j * per : (j + 1) * per, :]
        row_dt[j] = dt_ref[j * per : (j + 1) * per, :]
    bt[...] = jnp.transpose(b_ref[...].astype(F32)).astype(BF16)
    gram[...] = jnp.where(
        causal, lax.dot_general(c_ref[...], b_ref[...], NT, preferred_element_type=F32), 0.0
    )
    first = lax.broadcasted_iota(jnp.int32, (1, 128), 1) < HEAD_P

    @pl.when(me == 0)
    def _():
        arrived[...] = jnp.zeros_like(arrived)

    def lanes_of(j, pair):
        return pl.ds(pl.multiple_of(j * CHUNK + pair * 128, 128), 128)

    @pl.loop(0, chunks)
    def _(j):
        runs = col_run[j]
        steps = col_dt[j]
        for pair in range(CHUNK // 128):
            a = 2 * pair
            run = jnp.where(first, runs[:, a : a + 1], runs[:, a + 1 : a + 2])
            step = jnp.where(first, steps[:, a : a + 1], steps[:, a + 1 : a + 2])
            weighted = x_ref[:, lanes_of(j, pair)].astype(F32) * (
                jnp.exp(run[length - 1 : length, :] - run) * step
            )
            high, low = split(weighted)
            state[j, :, pair * 128 : (pair + 1) * 128] = dot(bt[...], high) + dot(bt[...], low)

        @pl.when(me == 0)
        def _():
            if n > 1:
                state_copy(j).start()

    q_acc[...] = jnp.zeros_like(q_acc)

    def add_query(part, weight):
        for t in range(0, q_cols, 512):
            q_acc[:, t : t + 512] += dot(part[...], weight[:, t : t + 512])

    def take_other(j):
        mixed_copy(j).wait_recv()
        weight_out(j).wait_recv()
        add_query(mixed_other.at[j], w_other.at[j])

    half = length // 2

    @pl.loop(0, chunks)
    def _(j):
        runs = col_run[j]

        @pl.when(has_left)
        def _():
            state_copy(j).wait_recv()

        @pl.when(has_left & has_right)
        def _():
            ends = runs[length - 1 : length, :]
            for pair in range(CHUNK // 128):
                a = 2 * pair
                keep = jnp.exp(jnp.where(first, ends[:, a : a + 1], ends[:, a + 1 : a + 2]))
                lanes = slice(pair * 128, (pair + 1) * 128)
                state[j, :, lanes] = keep * arrived[j, :, lanes] + state[j, :, lanes]
            state_copy(j).start()

        run_row = row_run[j]
        dt_row = row_dt[j]
        for pair in range(CHUNK // 128):
            lanes = lanes_of(j, pair)
            x_pair = x_ref[:, lanes]
            x_wide = x_pair.astype(F32)
            upper = jnp.zeros((half, 128), F32)
            lower = jnp.zeros((length - half, 128), F32)
            for member in range(2):
                a = 2 * pair + member
                x_own = jnp.where(first if member == 0 else ~first, x_wide, 0.0).astype(BF16)
                run_c = runs[:, a : a + 1]
                run_r = run_row[a : a + 1, :]
                dt_r = dt_row[a : a + 1, :]
                w_up = (
                    gram[:half, :half]
                    * jnp.exp(jnp.minimum(run_c[:half] - run_r[:, :half], 0.0))
                    * dt_r[:, :half]
                )
                high, low = split(w_up)
                upper = upper + dot(high, x_own[:half]) + dot(low, x_own[:half])
                w_low = gram[half:, :] * jnp.exp(jnp.minimum(run_c[half:] - run_r, 0.0)) * dt_r
                high, low = split(w_low)
                lower = lower + dot(high, x_own) + dot(low, x_own)
            high, low = split(arrived[j, :, pair * 128 : (pair + 1) * 128])
            carried = dot(c_ref[...], high) + dot(c_ref[...], low)
            a = 2 * pair
            grown = jnp.exp(jnp.where(first, runs[:, a : a + 1], runs[:, a + 1 : a + 2]))
            y = (
                jnp.concatenate([upper, lower], axis=0)
                + carried * grown
                + skip_ref[:, lanes] * x_wide
            )
            squares = y * y
            both = jnp.sum(squares, axis=1, keepdims=True)
            left = jnp.sum(jnp.where(first, squares, 0.0), axis=1, keepdims=True)
            right = jnp.sum(jnp.where(first, 0.0, squares), axis=1, keepdims=True)
            mean = jnp.where(first, left, right) * (1.0 / HEAD_P)
            out = (y * lax.rsqrt(mean + 1e-05) * gain_ref[:, lanes]).astype(BF16)
            mixed[j, :, pair * 128 : (pair + 1) * 128] = out
            mixer_ref[:, lanes] = out
        mixed_copy(j).start()
        weight_in(j).wait()
        add_query(mixed.at[j], w_own.at[j])

        @pl.when(j >= 1)
        def _():
            take_other(j - 1)

        @pl.when((j == 2) & has_left)
        def _():
            kv_wait(1)

        @pl.when((j == 2) & has_left & has_right)
        def _():
            kv_copy(1).start()

    take_other(chunks - 1)
    q_all[...] = q_acc[...].astype(BF16)
    top[...] = jnp.full_like(top, NEGATIVE)
    total[...] = jnp.zeros_like(total)
    acc[...] = jnp.zeros_like(acc)
    scale = HEAD_DIM ** (-0.5) * LOG2E

    def attend(slot):
        for i in range(blocks):
            for m in range(blocks):
                seen = mask_ref[me * blocks + i, (me - slot) * blocks + m] == 1
                bias[i * BLOCK : (i + 1) * BLOCK, m * BLOCK : (m + 1) * BLOCK] = jnp.full(
                    (BLOCK, BLOCK), jnp.where(seen, 0.0, NEGATIVE), F32
                )

        @pl.when(slot == 0)
        def _():
            same = (row // BLOCK) == (col // BLOCK)
            bias[...] = jnp.where(causal, jnp.where(same, 0.0, bias[...]), NEGATIVE)

        @pl.loop(0, heads)
        def _(h):
            mine = pl.ds(pl.multiple_of(h * HEAD_DIM, HEAD_DIM), HEAD_DIM)
            shared = pl.ds(pl.multiple_of((h // group) * HEAD_DIM, HEAD_DIM), HEAD_DIM)
            keys = kv[slot, 0, :, shared]
            values = kv[slot, 1, :, shared]
            scores = (
                lax.dot_general(q_all[:, mine], keys, NT, preferred_element_type=F32) + bias[...]
            )
            old_top = top[h]
            new_top = jnp.maximum(old_top, jnp.max(scores, axis=1, keepdims=True))
            fade = jnp.exp2((old_top - new_top) * scale)
            parts = [
                jnp.exp2((scores[:, t : t + 128] - new_top) * scale) for t in range(0, length, 128)
            ]
            summed = parts[0]
            for part in parts[1:]:
                summed = summed + part
            total[h] = total[h] * fade + summed
            weights = jnp.concatenate([part.astype(BF16) for part in parts], axis=1)
            acc[h] = acc[h] * fade + dot(weights, values)
            top[h] = new_top

    @pl.loop(0, n)
    def _(slot):
        @pl.when(slot <= me)
        def _():
            @pl.when(slot >= 2)
            def _():
                kv_wait(slot)

            @pl.when((slot >= 2) & has_right)
            def _():
                kv_copy(slot).start()

            attend(slot)

    @pl.loop(0, heads)
    def _(h):
        mine = pl.ds(pl.multiple_of(h * HEAD_DIM, HEAD_DIM), HEAD_DIM)
        attended_ref[:, mine] = (acc[h] / jnp.sum(total[h], axis=1, keepdims=True)).astype(BF16)

    @pl.loop(0, chunks)
    def _(j):
        mixed_copy(j).wait_send()
        weight_out(j).wait_send()

        @pl.when(has_right)
        def _():
            state_copy(j).wait_send()

    @pl.loop(0, n)
    def _(slot):
        @pl.when((slot <= me) & has_right)
        def _():
            kv_copy(slot).wait_send()


def on_device(
    ssm_input,
    input_map,
    output_map,
    step_size,
    log_decay,
    skip_gain,
    norm_gain,
    query_weight,
    key_states,
    value_states,
    block_mask,
):
    n = lax.axis_size("context")
    length, channels = ssm_input.shape
    q_cols = query_weight.shape[1] // lax.axis_size("tensor")
    chunks = channels // CHUNK
    heads = q_cols // HEAD_DIM
    per = CHUNK // HEAD_P
    kv_cols = key_states.shape[1]
    skip = jnp.repeat(skip_gain, HEAD_P).reshape(1, channels)
    vmem = pl.BlockSpec(memory_space=pltpu.VMEM)
    dma = pltpu.SemaphoreType.DMA
    out = jax.ShapeDtypeStruct((length, channels), BF16)
    return pl.pallas_call(
        functools.partial(kernel, n),
        out_shape=(out, jax.ShapeDtypeStruct((length, q_cols), BF16)),
        in_specs=[pl.BlockSpec(memory_space=pltpu.SMEM)]
        + [vmem] * 7
        + [pl.BlockSpec(memory_space=pl.ANY)]
        + [vmem] * 2,
        out_specs=(vmem, vmem),
        scratch_shapes=[
            pltpu.VMEM((n, 2, length, kv_cols), BF16),
            pltpu.VMEM((chunks, CHUNK, q_cols), BF16),
            pltpu.VMEM((chunks, CHUNK, q_cols), BF16),
            pltpu.VMEM((STATE, length), BF16),
            pltpu.VMEM((length, length), F32),
            pltpu.VMEM((chunks, length, per), F32),
            pltpu.VMEM((chunks, length, per), F32),
            pltpu.VMEM((chunks, per, length), F32),
            pltpu.VMEM((chunks, per, length), F32),
            pltpu.VMEM((chunks, STATE, CHUNK), F32),
            pltpu.VMEM((chunks, STATE, CHUNK), F32),
            pltpu.VMEM((chunks, length, CHUNK), BF16),
            pltpu.VMEM((chunks, length, CHUNK), BF16),
            pltpu.VMEM((length, q_cols), F32),
            pltpu.VMEM((length, q_cols), BF16),
            pltpu.VMEM((length, length), F32),
            pltpu.VMEM((heads, length, HEAD_DIM), F32),
            pltpu.VMEM((heads, length, HEAD_DIM), F32),
            pltpu.VMEM((heads, length, HEAD_DIM), F32),
            dma((n,)),
            dma((n + 1,)),
            dma((chunks,)),
            dma((chunks,)),
            dma((chunks,)),
            dma((chunks,)),
            dma((chunks,)),
            dma((chunks,)),
            dma((chunks,)),
        ],
        compiler_params=pltpu.CompilerParams(
            collective_id=0, has_side_effects=True, vmem_limit_bytes=56 * 1024 * 1024
        ),
        name="mixer_attention",
    )(
        block_mask,
        ssm_input,
        input_map,
        output_map,
        step_size,
        log_decay,
        skip,
        norm_gain.reshape(1, channels),
        query_weight,
        key_states,
        value_states,
    )


def solution(mesh):
    return jax.shard_map(
        on_device,
        mesh=mesh,
        in_specs=(
            P(("dp", "context"), "tensor"),
            P(("dp", "context"), None),
            P(("dp", "context"), None),
            P("tensor", ("dp", "context")),
            P("tensor", ("dp", "context")),
            P("tensor"),
            P("tensor"),
            P("tensor", None),
            P(("dp", "context"), "tensor"),
            P(("dp", "context"), "tensor"),
            P("dp", None),
        ),
        out_specs=(P(("dp", "context"), "tensor"), P(("dp", "context"), "tensor")),
        check_vma=False,
    )
```

```python
import functools

import jax
import jax.numpy as jnp
from jax import lax
from jax.experimental import pallas as pl
from jax.experimental.pallas import tpu as pltpu
from jax.sharding import PartitionSpec as P

HEAD_P = 64
STATE = 128
HEAD_DIM = 128
BLOCK = 128
CHUNK = 256
NEGATIVE = -1e30
LOG2E = 1.4426950408889634
HIGHEST = lax.Precision.HIGHEST
MESH = pl.DeviceIdType.MESH
F32 = jnp.float32
BF16 = jnp.bfloat16
NT = (((1,), (1,)), ((), ()))


def split(wide):
    high = wide.astype(BF16)
    rest = wide - high.astype(F32)
    middle = rest.astype(BF16)
    return high, middle, (rest - middle.astype(F32)).astype(BF16)


def dot(a, b):
    return jnp.dot(a, b, preferred_element_type=F32)


def dot_left(wide, narrow):
    high, middle, low = split(wide)
    return dot(high, narrow) + (dot(middle, narrow) + dot(low, narrow))


def dot_right(narrow, wide):
    high, middle, low = split(wide)
    return dot(narrow, high) + (dot(narrow, middle) + dot(narrow, low))


def kernel(
    n,
    mask_ref,
    x_ref,
    b_ref,
    c_ref,
    dt_ref,
    ld_ref,
    skip_ref,
    gain_ref,
    w_ref,
    k_ref,
    v_ref,
    mixer_ref,
    attended_ref,
    kv,
    w_own,
    w_other,
    bt,
    gram,
    col_run,
    col_dt,
    row_run,
    row_dt,
    state,
    arrived,
    mixed,
    mixed_other,
    q_acc,
    q_all,
    bias,
    weights,
    top,
    total,
    acc,
    kv_send,
    kv_recv,
    st_send,
    st_recv,
    mx_send,
    mx_recv,
    wt_send,
    wt_recv,
    wt_own,
):
    me = lax.axis_index("context")
    core = lax.axis_index("tensor")
    other = 1 - core
    length = x_ref.shape[0]
    chunks = x_ref.shape[1] // CHUNK
    q_cols = w_own.shape[2]
    has_left = me > 0
    has_right = me < n - 1
    heads = q_cols // HEAD_DIM
    group = heads // (k_ref.shape[1] // HEAD_DIM)
    blocks = length // BLOCK

    barrier = pltpu.get_barrier_semaphore()
    pl.semaphore_signal(barrier, inc=1, device_id={"tensor": other}, device_id_type=MESH)

    @pl.when(has_left)
    def _():
        pl.semaphore_signal(barrier, inc=1, device_id={"context": me - 1}, device_id_type=MESH)

    @pl.when(has_right)
    def _():
        pl.semaphore_signal(barrier, inc=1, device_id={"context": me + 1}, device_id_type=MESH)

    peers = 1 + has_left.astype(jnp.int32) + has_right.astype(jnp.int32)
    pl.semaphore_wait(barrier, peers)

    def pass_on(which, slot):
        return pltpu.make_async_remote_copy(
            src_ref=kv.at[which, slot],
            dst_ref=kv.at[which, slot + 1],
            send_sem=kv_send.at[which, slot],
            recv_sem=kv_recv.at[which, slot + 1],
            device_id={"context": me + 1},
            device_id_type=MESH,
        )

    def take(which, slot):
        @pl.when((slot >= 1) & (slot <= me))
        def _():
            pltpu.make_async_remote_copy(
                src_ref=kv.at[which, slot - 1],
                dst_ref=kv.at[which, slot],
                send_sem=kv_send.at[which, slot - 1],
                recv_sem=kv_recv.at[which, slot],
                device_id={"context": me - 1},
                device_id_type=MESH,
            ).wait_recv()

            @pl.when(has_right)
            def _():
                pass_on(which, slot).start()

    def state_copy(j):
        return pltpu.make_async_remote_copy(
            src_ref=state.at[j],
            dst_ref=arrived.at[j],
            send_sem=st_send.at[j],
            recv_sem=st_recv.at[j],
            device_id={"context": me + 1},
            device_id_type=MESH,
        )

    def mixed_copy(j):
        return pltpu.make_async_remote_copy(
            src_ref=mixed.at[j],
            dst_ref=mixed_other.at[j],
            send_sem=mx_send.at[j],
            recv_sem=mx_recv.at[j],
            device_id={"tensor": other},
            device_id_type=MESH,
        )

    def rows_of(j):
        return pl.ds(pl.multiple_of(j * CHUNK, CHUNK), CHUNK)

    def weight_out(j):
        return pltpu.make_async_remote_copy(
            src_ref=w_ref.at[rows_of(j), pl.ds(pl.multiple_of(other * q_cols, CHUNK), q_cols)],
            dst_ref=w_other.at[j],
            send_sem=wt_send.at[j],
            recv_sem=wt_recv.at[j],
            device_id={"tensor": other},
            device_id_type=MESH,
        )

    def weight_in(j):
        return pltpu.make_async_copy(
            w_ref.at[rows_of(j), pl.ds(pl.multiple_of(core * q_cols, CHUNK), q_cols)],
            w_own.at[j],
            wt_own.at[j],
        )

    kv[0, 0] = k_ref[...]
    kv[1, 0] = v_ref[...]

    @pl.when(has_left & has_right)
    def _():
        pass_on(0, 0).start()
        pass_on(1, 0).start()

    @pl.loop(0, chunks)
    def _(j):
        weight_in(j).start()
        weight_out(j).start()

    row = lax.broadcasted_iota(jnp.int32, (length, length), 0)
    col = lax.broadcasted_iota(jnp.int32, (length, length), 1)
    causal = row >= col
    tri = jnp.where(causal, 1.0, 0.0).astype(F32)
    eye = jnp.where(row == col, 1.0, 0.0).astype(F32)
    run_rows = lax.dot_general(ld_ref[...], tri, NT, precision=HIGHEST, preferred_element_type=F32)
    run_cols = lax.dot_general(tri, ld_ref[...], NT, precision=HIGHEST, preferred_element_type=F32)
    dt_cols = lax.dot_general(eye, dt_ref[...], NT, precision=HIGHEST, preferred_element_type=F32)
    per = CHUNK // HEAD_P
    for j in range(chunks):
        col_run[j] = run_cols[:, j * per : (j + 1) * per]
        col_dt[j] = dt_cols[:, j * per : (j + 1) * per]
        row_run[j] = run_rows[j * per : (j + 1) * per, :]
        row_dt[j] = dt_ref[j * per : (j + 1) * per, :]
    bt[...] = jnp.transpose(b_ref[...].astype(F32)).astype(BF16)
    gram[...] = jnp.where(
        causal, lax.dot_general(c_ref[...], b_ref[...], NT, preferred_element_type=F32), 0.0
    )
    first = lax.broadcasted_iota(jnp.int32, (1, 128), 1) < HEAD_P

    @pl.when(me == 0)
    def _():
        arrived[...] = jnp.zeros_like(arrived)

    def lanes_of(j, pair):
        return pl.ds(pl.multiple_of(j * CHUNK + pair * 128, 128), 128)

    @pl.loop(0, chunks)
    def _(j):
        runs = col_run[j]
        steps = col_dt[j]
        for pair in range(CHUNK // 128):
            a = 2 * pair
            run = jnp.where(first, runs[:, a : a + 1], runs[:, a + 1 : a + 2])
            step = jnp.where(first, steps[:, a : a + 1], steps[:, a + 1 : a + 2])
            weighted = x_ref[:, lanes_of(j, pair)].astype(F32) * (
                jnp.exp(run[length - 1 : length, :] - run) * step
            )
            state[j, :, pair * 128 : (pair + 1) * 128] = dot_right(bt[...], weighted)

        @pl.when(me == 0)
        def _():
            if n > 1:
                state_copy(j).start()

    @pl.when(me == 0)
    def _():
        if n > 1:
            pass_on(0, 0).start()
            pass_on(1, 0).start()

    same = (row // BLOCK) == (col // BLOCK)

    @pl.loop(0, n)
    def _(slot):
        @pl.when(slot <= me)
        def _():
            for i in range(blocks):
                for m in range(blocks):
                    seen = mask_ref[me * blocks + i, (me - slot) * blocks + m] == 1
                    bias[slot, i * BLOCK : (i + 1) * BLOCK, m * BLOCK : (m + 1) * BLOCK] = jnp.full(
                        (BLOCK, BLOCK), jnp.where(seen, 0.0, NEGATIVE), F32
                    )

    bias[0] = jnp.where(causal, jnp.where(same, 0.0, bias[0]), NEGATIVE)
    q_acc[...] = jnp.zeros_like(q_acc)

    def add_query(part, weight):
        for t in range(0, q_cols, 512):
            q_acc[:, t : t + 512] += dot(part[...], weight[:, t : t + 512])

    def take_other(j):
        mixed_copy(j).wait_recv()
        weight_out(j).wait_recv()
        add_query(mixed_other.at[j], w_other.at[j])

    half = length // 2

    @pl.loop(0, chunks)
    def _(j):
        runs = col_run[j]

        @pl.when(has_left)
        def _():
            state_copy(j).wait_recv()

        @pl.when(has_left & has_right)
        def _():
            ends = runs[length - 1 : length, :]
            for pair in range(CHUNK // 128):
                a = 2 * pair
                keep = jnp.exp(jnp.where(first, ends[:, a : a + 1], ends[:, a + 1 : a + 2]))
                lanes = slice(pair * 128, (pair + 1) * 128)
                state[j, :, lanes] = keep * arrived[j, :, lanes] + state[j, :, lanes]
            state_copy(j).start()

        run_row = row_run[j]
        dt_row = row_dt[j]
        for pair in range(CHUNK // 128):
            lanes = lanes_of(j, pair)
            x_pair = x_ref[:, lanes]
            x_wide = x_pair.astype(F32)
            upper = jnp.zeros((half, 128), F32)
            lower = jnp.zeros((length - half, 128), F32)
            for member in range(2):
                a = 2 * pair + member
                x_own = jnp.where(first if member == 0 else ~first, x_wide, 0.0).astype(BF16)
                run_c = runs[:, a : a + 1]
                run_r = run_row[a : a + 1, :]
                dt_r = dt_row[a : a + 1, :]
                w_up = (
                    gram[:half, :half]
                    * jnp.exp(jnp.minimum(run_c[:half] - run_r[:, :half], 0.0))
                    * dt_r[:, :half]
                )
                upper = upper + dot_left(w_up, x_own[:half])
                w_low = gram[half:, :] * jnp.exp(jnp.minimum(run_c[half:] - run_r, 0.0)) * dt_r
                lower = lower + dot_left(w_low, x_own)
            carried = dot_right(c_ref[...], arrived[j, :, pair * 128 : (pair + 1) * 128])
            a = 2 * pair
            grown = jnp.exp(jnp.where(first, runs[:, a : a + 1], runs[:, a + 1 : a + 2]))
            y = (
                jnp.concatenate([upper, lower], axis=0)
                + carried * grown
                + jnp.where(first, skip_ref[j * per + a], skip_ref[j * per + a + 1]) * x_wide
            )
            squares = y * y
            both = jnp.sum(squares, axis=1, keepdims=True)
            left = jnp.sum(jnp.where(first, squares, 0.0), axis=1, keepdims=True)
            right = jnp.sum(jnp.where(first, 0.0, squares), axis=1, keepdims=True)
            mean = jnp.where(first, left, right) * (1.0 / HEAD_P)
            out = (y * lax.rsqrt(mean + 1e-05) * gain_ref[:, lanes]).astype(BF16)
            mixed[j, :, pair * 128 : (pair + 1) * 128] = out
            mixer_ref[:, lanes] = out
        mixed_copy(j).start()
        weight_in(j).wait()
        add_query(mixed.at[j], w_own.at[j])

        @pl.when(j >= 1)
        def _():
            take_other(j - 1)

    take_other(chunks - 1)

    @pl.when(has_right)
    def _():
        for which in range(2):

            @pl.loop(1, n)
            def _(slot, which=which):
                take(which, slot)

    q_all[...] = q_acc[...].astype(BF16)
    top[...] = jnp.full_like(top, NEGATIVE)
    total[...] = jnp.zeros_like(total)
    acc[...] = jnp.zeros_like(acc)
    scale = HEAD_DIM ** (-0.5) * LOG2E

    def head_lanes(h):
        return pl.ds(pl.multiple_of(h * HEAD_DIM, HEAD_DIM), HEAD_DIM)

    def scores_of(slot, h, keys):
        return (
            lax.dot_general(q_all[:, head_lanes(h)], keys, NT, preferred_element_type=F32)
            + bias[slot]
        )

    @pl.loop(0, n)
    def _(slot):
        @pl.when(slot <= me)
        def _():
            @pl.when(~has_right)
            def _():
                take(0, slot)

            @pl.loop(0, heads // group)
            def _(g):
                keys = kv[0, slot, :, head_lanes(g)]
                for member in range(group):
                    h = g * group + member
                    scores = scores_of(slot, h, keys)
                    best = top[h]
                    for t in range(0, length, 128):
                        best = jnp.maximum(best, scores[:, t : t + 128])
                    top[h] = best

    @pl.loop(0, heads)
    def _(h):
        top[h] = jnp.broadcast_to(jnp.max(top[h], axis=1, keepdims=True), top.shape[1:])

    @pl.loop(0, n)
    def _(slot):
        @pl.when(slot <= me)
        def _():
            @pl.loop(0, heads // group)
            def _(g):
                keys = kv[0, slot, :, head_lanes(g)]
                for member in range(group):
                    h = g * group + member
                    scores = scores_of(slot, h, keys)
                    best = top[h]
                    summed = total[h]
                    for t in range(0, length, 128):
                        part = jnp.exp2((scores[:, t : t + 128] - best) * scale)
                        summed = summed + part
                        weights[h, :, t : t + 128] = part.astype(BF16)
                    total[h] = summed

            @pl.when(~has_right)
            def _():
                take(1, slot)

            @pl.loop(0, heads // group)
            def _(g):
                values = kv[1, slot, :, head_lanes(g)]
                for member in range(group):
                    h = g * group + member
                    acc[h] += dot(weights[h], values)

    @pl.loop(0, heads)
    def _(h):
        attended_ref[:, head_lanes(h)] = (
            acc[h] / jnp.sum(total[h], axis=1, keepdims=True)
        ).astype(BF16)

    @pl.loop(0, chunks)
    def _(j):
        mixed_copy(j).wait_send()
        weight_out(j).wait_send()

        @pl.when(has_right)
        def _():
            state_copy(j).wait_send()

    @pl.loop(0, n)
    def _(slot):
        @pl.when((slot <= me) & has_right)
        def _():
            pass_on(0, slot).wait_send()
            pass_on(1, slot).wait_send()


def on_device(
    ssm_input,
    input_map,
    output_map,
    step_size,
    log_decay,
    skip_gain,
    norm_gain,
    query_weight,
    key_states,
    value_states,
    block_mask,
):
    n = lax.axis_size("context")
    length, channels = ssm_input.shape
    q_cols = query_weight.shape[1] // lax.axis_size("tensor")
    chunks = channels // CHUNK
    heads = q_cols // HEAD_DIM
    per = CHUNK // HEAD_P
    kv_cols = key_states.shape[1]
    vmem = pl.BlockSpec(memory_space=pltpu.VMEM)
    smem = pl.BlockSpec(memory_space=pltpu.SMEM)
    dma = pltpu.SemaphoreType.DMA
    out = jax.ShapeDtypeStruct((length, channels), BF16)
    return pl.pallas_call(
        functools.partial(kernel, n),
        out_shape=(out, jax.ShapeDtypeStruct((length, q_cols), BF16)),
        in_specs=[smem]
        + [vmem] * 5
        + [smem, vmem]
        + [pl.BlockSpec(memory_space=pl.ANY)]
        + [vmem] * 2,
        out_specs=(vmem, vmem),
        scratch_shapes=[
            pltpu.VMEM((2, n, length, kv_cols), BF16),
            pltpu.VMEM((chunks, CHUNK, q_cols), BF16),
            pltpu.VMEM((chunks, CHUNK, q_cols), BF16),
            pltpu.VMEM((STATE, length), BF16),
            pltpu.VMEM((length, length), F32),
            pltpu.VMEM((chunks, length, per), F32),
            pltpu.VMEM((chunks, length, per), F32),
            pltpu.VMEM((chunks, per, length), F32),
            pltpu.VMEM((chunks, per, length), F32),
            pltpu.VMEM((chunks, STATE, CHUNK), F32),
            pltpu.VMEM((chunks, STATE, CHUNK), F32),
            pltpu.VMEM((chunks, length, CHUNK), BF16),
            pltpu.VMEM((chunks, length, CHUNK), BF16),
            pltpu.VMEM((length, q_cols), F32),
            pltpu.VMEM((length, q_cols), BF16),
            pltpu.VMEM((n, length, length), F32),
            pltpu.VMEM((heads, length, length), BF16),
            pltpu.VMEM((heads, length, HEAD_DIM), F32),
            pltpu.VMEM((heads, length, HEAD_DIM), F32),
            pltpu.VMEM((heads, length, HEAD_DIM), F32),
            dma((2, n)),
            dma((2, n + 1)),
            dma((chunks,)),
            dma((chunks,)),
            dma((chunks,)),
            dma((chunks,)),
            dma((chunks,)),
            dma((chunks,)),
            dma((chunks,)),
        ],
        compiler_params=pltpu.CompilerParams(
            collective_id=0, has_side_effects=True, vmem_limit_bytes=56 * 1024 * 1024
        ),
        name="mixer_attention",
    )(
        block_mask,
        ssm_input,
        input_map,
        output_map,
        step_size,
        log_decay,
        skip_gain,
        norm_gain.reshape(1, channels),
        query_weight,
        key_states,
        value_states,
    )


def solution(mesh):
    return jax.shard_map(
        on_device,
        mesh=mesh,
        in_specs=(
            P(("dp", "context"), "tensor"),
            P(("dp", "context"), None),
            P(("dp", "context"), None),
            P("tensor", ("dp", "context")),
            P("tensor", ("dp", "context")),
            P("tensor"),
            P("tensor"),
            P("tensor", None),
            P(("dp", "context"), "tensor"),
            P(("dp", "context"), "tensor"),
            P("dp", None),
        ),
        out_specs=(P(("dp", "context"), "tensor"), P(("dp", "context"), "tensor")),
        check_vma=False,
    )
```

```python
import functools

import jax
import jax.numpy as jnp
from jax import lax
from jax.experimental import pallas as pl
from jax.experimental.pallas import tpu as pltpu
from jax.sharding import PartitionSpec as P

HEAD_P = 64
STATE = 128
HEAD_DIM = 128
BLOCK = 128
CHUNK = 256
NEGATIVE = -1e30
LOG2E = 1.4426950408889634
HIGHEST = lax.Precision.HIGHEST
MESH = pl.DeviceIdType.MESH
F32 = jnp.float32
BF16 = jnp.bfloat16
NT = (((1,), (1,)), ((), ()))


def split(wide):
    high = wide.astype(BF16)
    rest = wide - high.astype(F32)
    middle = rest.astype(BF16)
    return high, middle, (rest - middle.astype(F32)).astype(BF16)


def dot(a, b):
    return jnp.dot(a, b, preferred_element_type=F32)


def dot_left(wide, narrow):
    high, middle, low = split(wide)
    return dot(high, narrow) + (dot(middle, narrow) + dot(low, narrow))


def dot_right(narrow, wide):
    high, middle, low = split(wide)
    return dot(narrow, high) + (dot(narrow, middle) + dot(narrow, low))


def kernel(
    n,
    mask_ref,
    x_ref,
    b_ref,
    c_ref,
    dt_ref,
    ld_ref,
    skip_ref,
    gain_ref,
    w_ref,
    k_ref,
    v_ref,
    mixer_ref,
    attended_ref,
    kv,
    w_own,
    w_other,
    bt,
    gram,
    col_run,
    col_dt,
    row_run,
    row_dt,
    state,
    arrived,
    mixed,
    mixed_other,
    q_acc,
    q_all,
    bias,
    weights,
    top,
    total,
    acc,
    kv_send,
    kv_recv,
    st_send,
    st_recv,
    mx_send,
    mx_recv,
    wt_send,
    wt_recv,
    wt_own,
):
    me = lax.axis_index("context")
    core = lax.axis_index("tensor")
    other = 1 - core
    length = x_ref.shape[0]
    chunks = x_ref.shape[1] // CHUNK
    q_cols = w_own.shape[2]
    has_left = me > 0
    has_right = me < n - 1
    heads = q_cols // HEAD_DIM
    group = heads // (k_ref.shape[1] // HEAD_DIM)
    blocks = length // BLOCK

    barrier = pltpu.get_barrier_semaphore()
    pl.semaphore_signal(barrier, inc=1, device_id={"tensor": other}, device_id_type=MESH)

    @pl.when(has_left)
    def _():
        pl.semaphore_signal(barrier, inc=1, device_id={"context": me - 1}, device_id_type=MESH)

    @pl.when(has_right)
    def _():
        pl.semaphore_signal(barrier, inc=1, device_id={"context": me + 1}, device_id_type=MESH)

    peers = 1 + has_left.astype(jnp.int32) + has_right.astype(jnp.int32)
    pl.semaphore_wait(barrier, peers)

    def pass_on(which, slot):
        return pltpu.make_async_remote_copy(
            src_ref=kv.at[which, slot],
            dst_ref=kv.at[which, slot + 1],
            send_sem=kv_send.at[which, slot],
            recv_sem=kv_recv.at[which, slot + 1],
            device_id={"context": me + 1},
            device_id_type=MESH,
        )

    def take(which, slot):
        @pl.when((slot >= 1) & (slot <= me))
        def _():
            pltpu.make_async_remote_copy(
                src_ref=kv.at[which, slot - 1],
                dst_ref=kv.at[which, slot],
                send_sem=kv_send.at[which, slot - 1],
                recv_sem=kv_recv.at[which, slot],
                device_id={"context": me - 1},
                device_id_type=MESH,
            ).wait_recv()

            @pl.when(has_right)
            def _():
                pass_on(which, slot).start()

    def state_copy(j):
        return pltpu.make_async_remote_copy(
            src_ref=state.at[j],
            dst_ref=arrived.at[j],
            send_sem=st_send.at[j],
            recv_sem=st_recv.at[j],
            device_id={"context": me + 1},
            device_id_type=MESH,
        )

    def mixed_copy(j):
        return pltpu.make_async_remote_copy(
            src_ref=mixed.at[j],
            dst_ref=mixed_other.at[j],
            send_sem=mx_send.at[j],
            recv_sem=mx_recv.at[j],
            device_id={"tensor": other},
            device_id_type=MESH,
        )

    def rows_of(j):
        return pl.ds(pl.multiple_of(j * CHUNK, CHUNK), CHUNK)

    def weight_out(j):
        return pltpu.make_async_remote_copy(
            src_ref=w_ref.at[rows_of(j), pl.ds(pl.multiple_of(other * q_cols, CHUNK), q_cols)],
            dst_ref=w_other.at[j],
            send_sem=wt_send.at[j],
            recv_sem=wt_recv.at[j],
            device_id={"tensor": other},
            device_id_type=MESH,
        )

    def weight_in(j):
        return pltpu.make_async_copy(
            w_ref.at[rows_of(j), pl.ds(pl.multiple_of(core * q_cols, CHUNK), q_cols)],
            w_own.at[j],
            wt_own.at[j],
        )

    kv[0, 0] = k_ref[...]
    kv[1, 0] = v_ref[...]

    @pl.when(has_left & has_right)
    def _():
        pass_on(0, 0).start()
        pass_on(1, 0).start()

    @pl.loop(0, chunks)
    def _(j):
        weight_in(j).start()
        weight_out(j).start()

    row = lax.broadcasted_iota(jnp.int32, (length, length), 0)
    col = lax.broadcasted_iota(jnp.int32, (length, length), 1)
    causal = row >= col
    tri = jnp.where(causal, 1.0, 0.0).astype(F32)
    eye = jnp.where(row == col, 1.0, 0.0).astype(F32)
    run_rows = lax.dot_general(ld_ref[...], tri, NT, precision=HIGHEST, preferred_element_type=F32)
    run_cols = lax.dot_general(tri, ld_ref[...], NT, precision=HIGHEST, preferred_element_type=F32)
    dt_cols = lax.dot_general(eye, dt_ref[...], NT, precision=HIGHEST, preferred_element_type=F32)
    per = CHUNK // HEAD_P
    for j in range(chunks):
        col_run[j] = run_cols[:, j * per : (j + 1) * per]
        col_dt[j] = dt_cols[:, j * per : (j + 1) * per]
        row_run[j] = run_rows[j * per : (j + 1) * per, :]
        row_dt[j] = dt_ref[j * per : (j + 1) * per, :]
    bt[...] = jnp.transpose(b_ref[...].astype(F32)).astype(BF16)
    gram[...] = jnp.where(
        causal, lax.dot_general(c_ref[...], b_ref[...], NT, preferred_element_type=F32), 0.0
    )
    first = lax.broadcasted_iota(jnp.int32, (1, 128), 1) < HEAD_P

    @pl.when(me == 0)
    def _():
        arrived[...] = jnp.zeros_like(arrived)

    def lanes_of(j, pair):
        return pl.ds(pl.multiple_of(j * CHUNK + pair * 128, 128), 128)

    @pl.loop(0, chunks)
    def _(j):
        runs = col_run[j]
        steps = col_dt[j]
        for pair in range(CHUNK // 128):
            a = 2 * pair
            run = jnp.where(first, runs[:, a : a + 1], runs[:, a + 1 : a + 2])
            step = jnp.where(first, steps[:, a : a + 1], steps[:, a + 1 : a + 2])
            weighted = x_ref[:, lanes_of(j, pair)].astype(F32) * (
                jnp.exp(run[length - 1 : length, :] - run) * step
            )
            state[j, :, pair * 128 : (pair + 1) * 128] = dot_right(bt[...], weighted)

        @pl.when(me == 0)
        def _():
            if n > 1:
                state_copy(j).start()

    @pl.when(me == 0)
    def _():
        if n > 1:
            pass_on(0, 0).start()
            pass_on(1, 0).start()

    same = (row // BLOCK) == (col // BLOCK)

    @pl.loop(0, n)
    def _(slot):
        @pl.when(slot <= me)
        def _():
            for i in range(blocks):
                for m in range(blocks):
                    seen = mask_ref[me * blocks + i, (me - slot) * blocks + m] == 1
                    bias[slot, i * BLOCK : (i + 1) * BLOCK, m * BLOCK : (m + 1) * BLOCK] = jnp.full(
                        (BLOCK, BLOCK), jnp.where(seen, 0.0, NEGATIVE), F32
                    )

    bias[0] = jnp.where(causal, jnp.where(same, 0.0, bias[0]), NEGATIVE)
    q_acc[...] = jnp.zeros_like(q_acc)

    def add_query(part, weight):
        for t in range(0, q_cols, 512):
            q_acc[:, t : t + 512] += dot(part[...], weight[:, t : t + 512])

    def take_other(j):
        mixed_copy(j).wait_recv()
        weight_out(j).wait_recv()
        add_query(mixed_other.at[j], w_other.at[j])

    half = length // 2

    @pl.when(me >= 2)
    def _():
        take(0, 1)

    @pl.loop(0, chunks)
    def _(j):
        runs = col_run[j]

        @pl.when(has_left)
        def _():
            state_copy(j).wait_recv()

        @pl.when(has_left & has_right)
        def _():
            ends = runs[length - 1 : length, :]
            for pair in range(CHUNK // 128):
                a = 2 * pair
                keep = jnp.exp(jnp.where(first, ends[:, a : a + 1], ends[:, a + 1 : a + 2]))
                lanes = slice(pair * 128, (pair + 1) * 128)
                state[j, :, lanes] = keep * arrived[j, :, lanes] + state[j, :, lanes]
            state_copy(j).start()

        run_row = row_run[j]
        dt_row = row_dt[j]
        for pair in range(CHUNK // 128):
            lanes = lanes_of(j, pair)
            x_pair = x_ref[:, lanes]
            x_wide = x_pair.astype(F32)
            upper = jnp.zeros((half, 128), F32)
            lower = jnp.zeros((length - half, 128), F32)
            for member in range(2):
                a = 2 * pair + member
                x_own = jnp.where(first if member == 0 else ~first, x_wide, 0.0).astype(BF16)
                run_c = runs[:, a : a + 1]
                run_r = run_row[a : a + 1, :]
                dt_r = dt_row[a : a + 1, :]
                w_up = (
                    gram[:half, :half]
                    * jnp.exp(jnp.minimum(run_c[:half] - run_r[:, :half], 0.0))
                    * dt_r[:, :half]
                )
                upper = upper + dot_left(w_up, x_own[:half])
                w_low = gram[half:, :] * jnp.exp(jnp.minimum(run_c[half:] - run_r, 0.0)) * dt_r
                lower = lower + dot_left(w_low, x_own)
            carried = dot_right(c_ref[...], arrived[j, :, pair * 128 : (pair + 1) * 128])
            a = 2 * pair
            grown = jnp.exp(jnp.where(first, runs[:, a : a + 1], runs[:, a + 1 : a + 2]))
            y = (
                jnp.concatenate([upper, lower], axis=0)
                + carried * grown
                + jnp.where(first, skip_ref[j * per + a], skip_ref[j * per + a + 1]) * x_wide
            )
            squares = y * y
            both = jnp.sum(squares, axis=1, keepdims=True)
            left = jnp.sum(jnp.where(first, squares, 0.0), axis=1, keepdims=True)
            right = jnp.sum(jnp.where(first, 0.0, squares), axis=1, keepdims=True)
            mean = jnp.where(first, left, right) * (1.0 / HEAD_P)
            out = (y * lax.rsqrt(mean + 1e-05) * gain_ref[:, lanes]).astype(BF16)
            mixed[j, :, pair * 128 : (pair + 1) * 128] = out
            mixer_ref[:, lanes] = out
        mixed_copy(j).start()
        weight_in(j).wait()
        add_query(mixed.at[j], w_own.at[j])

        @pl.when(j >= 1)
        def _():
            take_other(j - 1)

    take_other(chunks - 1)

    @pl.when(has_right)
    def _():
        for which in range(2):

            @pl.loop(1, n)
            def _(slot, which=which):
                @pl.when((which == 1) | (slot >= 2) | (me < 2))
                def _():
                    take(which, slot)

    q_all[...] = q_acc[...].astype(BF16)
    top[...] = jnp.full_like(top, NEGATIVE)
    total[...] = jnp.zeros_like(total)
    acc[...] = jnp.zeros_like(acc)
    scale = HEAD_DIM ** (-0.5) * LOG2E

    def head_lanes(h):
        return pl.ds(pl.multiple_of(h * HEAD_DIM, HEAD_DIM), HEAD_DIM)

    def scores_of(slot, h, keys):
        return (
            lax.dot_general(q_all[:, head_lanes(h)], keys, NT, preferred_element_type=F32)
            + bias[slot]
        )

    @pl.loop(0, n)
    def _(slot):
        @pl.when(slot <= me)
        def _():
            @pl.when(~has_right & ((slot >= 2) | (me < 2)))
            def _():
                take(0, slot)

            @pl.loop(0, heads // group)
            def _(g):
                keys = kv[0, slot, :, head_lanes(g)]
                for member in range(group):
                    h = g * group + member
                    scores = scores_of(slot, h, keys)
                    best = top[h]
                    for t in range(0, length, 128):
                        best = jnp.maximum(best, scores[:, t : t + 128])
                    top[h] = best

    @pl.loop(0, heads)
    def _(h):
        top[h] = jnp.broadcast_to(jnp.max(top[h], axis=1, keepdims=True), top.shape[1:])

    @pl.loop(0, n)
    def _(slot):
        @pl.when(slot <= me)
        def _():
            @pl.loop(0, heads // group)
            def _(g):
                keys = kv[0, slot, :, head_lanes(g)]
                for member in range(group):
                    h = g * group + member
                    scores = scores_of(slot, h, keys)
                    best = top[h]
                    summed = total[h]
                    for t in range(0, length, 128):
                        part = jnp.exp2((scores[:, t : t + 128] - best) * scale)
                        summed = summed + part
                        weights[h, :, t : t + 128] = part.astype(BF16)
                    total[h] = summed

            @pl.when(~has_right)
            def _():
                take(1, slot)

            @pl.loop(0, heads // group)
            def _(g):
                values = kv[1, slot, :, head_lanes(g)]
                for member in range(group):
                    h = g * group + member
                    acc[h] += dot(weights[h], values)

    @pl.loop(0, heads)
    def _(h):
        attended_ref[:, head_lanes(h)] = (
            acc[h] / jnp.sum(total[h], axis=1, keepdims=True)
        ).astype(BF16)

    @pl.loop(0, chunks)
    def _(j):
        mixed_copy(j).wait_send()
        weight_out(j).wait_send()

        @pl.when(has_right)
        def _():
            state_copy(j).wait_send()

    @pl.loop(0, n)
    def _(slot):
        @pl.when((slot <= me) & has_right)
        def _():
            pass_on(0, slot).wait_send()
            pass_on(1, slot).wait_send()


def hand_on(mixer_ref, attended_ref, mixer_out, attended_out):
    mixer_out[...] = mixer_ref[...]
    attended_out[...] = attended_ref[...]


def on_device(
    ssm_input,
    input_map,
    output_map,
    step_size,
    log_decay,
    skip_gain,
    norm_gain,
    query_weight,
    key_states,
    value_states,
    block_mask,
):
    n = lax.axis_size("context")
    length, channels = ssm_input.shape
    q_cols = query_weight.shape[1] // lax.axis_size("tensor")
    chunks = channels // CHUNK
    heads = q_cols // HEAD_DIM
    per = CHUNK // HEAD_P
    kv_cols = key_states.shape[1]
    vmem = pl.BlockSpec(memory_space=pltpu.VMEM)
    smem = pl.BlockSpec(memory_space=pltpu.SMEM)
    dma = pltpu.SemaphoreType.DMA
    out = jax.ShapeDtypeStruct((length, channels), BF16)
    results = pl.pallas_call(
        functools.partial(kernel, n),
        out_shape=(out, jax.ShapeDtypeStruct((length, q_cols), BF16)),
        in_specs=[smem]
        + [vmem] * 5
        + [smem, vmem]
        + [pl.BlockSpec(memory_space=pl.ANY)]
        + [vmem] * 2,
        out_specs=(vmem, vmem),
        scratch_shapes=[
            pltpu.VMEM((2, n, length, kv_cols), BF16),
            pltpu.VMEM((chunks, CHUNK, q_cols), BF16),
            pltpu.VMEM((chunks, CHUNK, q_cols), BF16),
            pltpu.VMEM((STATE, length), BF16),
            pltpu.VMEM((length, length), F32),
            pltpu.VMEM((chunks, length, per), F32),
            pltpu.VMEM((chunks, length, per), F32),
            pltpu.VMEM((chunks, per, length), F32),
            pltpu.VMEM((chunks, per, length), F32),
            pltpu.VMEM((chunks, STATE, CHUNK), F32),
            pltpu.VMEM((chunks, STATE, CHUNK), F32),
            pltpu.VMEM((chunks, length, CHUNK), BF16),
            pltpu.VMEM((chunks, length, CHUNK), BF16),
            pltpu.VMEM((length, q_cols), F32),
            pltpu.VMEM((length, q_cols), BF16),
            pltpu.VMEM((n, length, length), F32),
            pltpu.VMEM((heads, length, length), BF16),
            pltpu.VMEM((heads, length, HEAD_DIM), F32),
            pltpu.VMEM((heads, length, HEAD_DIM), F32),
            pltpu.VMEM((heads, length, HEAD_DIM), F32),
            dma((2, n)),
            dma((2, n + 1)),
            dma((chunks,)),
            dma((chunks,)),
            dma((chunks,)),
            dma((chunks,)),
            dma((chunks,)),
            dma((chunks,)),
            dma((chunks,)),
        ],
        compiler_params=pltpu.CompilerParams(
            collective_id=0, has_side_effects=True, vmem_limit_bytes=56 * 1024 * 1024
        ),
        name="mixer_attention",
    )(
        block_mask,
        ssm_input,
        input_map,
        output_map,
        step_size,
        log_decay,
        skip_gain,
        norm_gain.reshape(1, channels),
        query_weight,
        key_states,
        value_states,
    )
    rows = length // 4
    blocks = [
        pl.BlockSpec((rows, channels), lambda i: (i, 0)),
        pl.BlockSpec((rows, q_cols), lambda i: (i, 0)),
    ]
    return pl.pallas_call(
        hand_on,
        out_shape=(out, jax.ShapeDtypeStruct((length, q_cols), BF16)),
        grid=(4,),
        in_specs=blocks,
        out_specs=blocks,
        name="hand_on",
    )(*results)


def solution(mesh):
    return jax.shard_map(
        on_device,
        mesh=mesh,
        in_specs=(
            P(("dp", "context"), "tensor"),
            P(("dp", "context"), None),
            P(("dp", "context"), None),
            P("tensor", ("dp", "context")),
            P("tensor", ("dp", "context")),
            P("tensor"),
            P("tensor"),
            P("tensor", None),
            P(("dp", "context"), "tensor"),
            P(("dp", "context"), "tensor"),
            P("dp", None),
        ),
        out_specs=(P(("dp", "context"), "tensor"), P(("dp", "context"), "tensor")),
        check_vma=False,
    )
```
